256 devices in a mesh: section: 8 (over y_lo, x), expert: 8 (over z), tensor: 4 (over y_hi, core).
Axes of the slice: x: 4, y: 4 (y_hi: 2, y_lo: 2; y = y_hi * 2 + y_lo), z: 8, core: 2. Of those that a mesh axis runs over, the one named last changes fastest.
Arguments:
- slab: bfloat16 [8, 1536, 7168], P('section', ('expert', 'tensor')), may hold values from -6 to 6
- route_ids: int32 [8, 1536, 2], P('section', ('expert', 'tensor')), may hold values from 0 to 7, all different within a row; in each aligned block of 48 rows (0 to 47, 48 to 95, ..., all dimensions but the last counted through in order) at most 24 rows name the same one
- route_weights: float32 [8, 1536, 2], P('section', ('expert', 'tensor')), may hold values from 0.1 to 1
- norm_gain: float32 [8, 7168], P('section'), may hold values from 0.25 to 1.75
- w_gate: bfloat16 [8, 8, 7168, 1024], P('section', 'expert', None, 'tensor'), may hold values from -0.0625 to 0.0625
- w_up: bfloat16 [8, 8, 7168, 1024], P('section', 'expert', None, 'tensor'), may hold values from -0.0625 to 0.0625
- w_down: bfloat16 [8, 8, 1024, 7168], P('section', 'expert', 'tensor'), may hold values from -0.1875 to 0.1875
Outputs:
- next_slab: bfloat16 [8, 1536, 7168], P('section', ('expert', 'tensor'))
The draws below stay inside these ranges and needn't reach their ends.
Inputs may be any that keep to these rules, and one draw needn't show every extreme that they name: `route_ids`: within the rows of one device (aligned blocks of 48 token rows) no expert is named by more than 24 rows, a bound that some block reaches. The ids of a row differ.
All inputs are finite; a program needn't handle non-finite values.
Results may differ from the reference program's by a relative error of at most 0.006.
Values may be sent and summed in bfloat16 or wider, within the bound.
No kernel may reach another device: no remote copies, remote signals or barrier semaphores. Data moves between devices by JAX's collectives and lax.ppermute only.
A program may use at most 128 MiB of HBM per device.

```python
import math
import jax
import jax.numpy as jnp
import numpy as np
from jax import lax

D = 7168
FF = 1024
TOPK = 2
TOK_DEV = 48
EXPERTS = 8
FFD = 256
CAP = 24
TOKENS = 1536
N_SECTION = 8
N_EXPERT = 8
N_TENSOR = 4


def steps_of(stream_key, dims, pieces, smallest, high):
    def one(position, blocks):
        draws = jax.random.uniform(jax.random.fold_in(jax.random.fold_in(stream_key, 6), position), (blocks,), jnp.float32, smallest / len(pieces), high / len(pieces))
        return jnp.repeat(jnp.exp(draws), dims[position] // blocks).reshape((-1,) + (1,) * (len(dims) - position - 1))

    level = one(*pieces[0])
    for cut in pieces[1:]:
        level = level * one(*cut)
    return level


def assign_block(rng, own, number, rows, count, top, bound, skew):
    ranking = jax.random.permutation(rng, count)
    heavy_load, common = portions_of(count, rows * top, bound, skew, True), portions_of(count, rows * top, bound, skew, False)
    places = jnp.arange(count)

    def named(sizes, rotation):
        used = int((sizes > 0).sum())
        fixed = max(1, used // 4)
        moved = fixed + (places - fixed + rotation * (used - fixed)) % max(1, count - fixed)
        return jnp.zeros((count,), jnp.int32).at[ranking[jnp.where(places < fixed, places, moved)]].set(jnp.asarray(sizes, jnp.int32))

    sizes = jnp.where(number % 4 == 0, named(heavy_load, number // 4), named(common, number - number // 4 - 1))
    mixed = jax.random.permutation(jax.random.fold_in(own, 3), count)
    source_of, receiver = mixed[0:count // 2 * 2:2], mixed[1:count // 2 * 2:2]
    room = jnp.minimum(sizes[source_of] - 1, bound - sizes[receiver]) // 2
    room = jnp.where((source_of == ranking[0]) | (receiver == ranking[0]) | (sizes[receiver] == 0), 0, jnp.maximum(room, 0))
    moved = jax.random.randint(jax.random.fold_in(own, 4), (count // 2,), 0, 1 << 20) % (room + 1)
    sizes = sizes.at[source_of].add(-moved).at[receiver].add(moved)
    labels = jnp.searchsorted(jnp.cumsum(sizes), jnp.arange(rows * top), side="right").astype(jnp.int32)
    table = labels.reshape(top, rows).T
    table = table[jax.random.permutation(jax.random.fold_in(own, 1), rows)]
    rotation = jax.random.randint(jax.random.fold_in(own, 2), (rows, 1), 0, top)
    return jnp.take_along_axis(table, (jnp.arange(top)[None, :] + rotation) % top, axis=1)


def portions_of(amount, total, reach, slope, full):
    weights = [(1 << 20) // math.isqrt(standing ** slope) + 1 for standing in range(1, amount + 1)]
    largest = reach if full else min(reach, max(-(-total // amount), total * weights[0] // sum(weights)))
    least = 1 if total - largest >= amount - 1 else 0
    holding, spare = [largest] + [least] * (amount - 1), total - largest - least * (amount - 1)
    while spare > 0:
        movable = [i for i in range(1, amount) if holding[i] < largest] or [i for i in range(1, amount) if holding[i] < reach]
        pool, left = sum([weights[i] for i in movable]), spare
        for i in movable:
            addition = min(reach - holding[i], max(1, left * weights[i] // pool), spare)
            holding[i] = holding[i] + addition
            spare = spare - addition
    return np.array(holding)


def noise(rng, dims, scale, limit, pieces=(), kind=jnp.bfloat16):
    result = scale * jax.random.normal(rng, dims, jnp.float32)
    if pieces:
        result = result * steps_of(rng, dims, pieces, -0.22, 0.18)
    return jnp.clip(result, -limit, limit).astype(kind)


def setup_inputs(seed: int = 0) -> dict:
    key_list = jax.random.split(jax.random.key(seed), 8)
    slab = noise(key_list[0], (N_SECTION, TOKENS, D), 1.0, 6.0, ((0, 8), (1, 32)))
    route_ids_keys = jax.random.split(jax.random.fold_in(key_list[1], 1), N_SECTION * TOKENS // TOK_DEV)
    route_ids_turns = jax.random.permutation(jax.random.fold_in(key_list[1], 3), N_SECTION * TOKENS // TOK_DEV)
    route_ids = jax.vmap(lambda own, number: assign_block(jax.random.fold_in(key_list[1], 2), own, number, TOK_DEV, EXPERTS, TOPK, CAP, 2))(route_ids_keys, route_ids_turns).reshape((N_SECTION, TOKENS, TOPK))
    route_weights = jnp.clip(0.1 + 0.9 * jax.random.uniform(key_list[2], (N_SECTION, TOKENS, TOPK), jnp.float32) ** steps_of(key_list[2], (N_SECTION, TOKENS, TOPK), ((0, 8), (1, 32)), -0.2, 0.2), 0.1, 1.0)
    norm_gain = jnp.clip(1.0 + 0.15 * jax.random.normal(key_list[3], (N_SECTION, D), jnp.float32), 0.25, 1.75)
    w_gate = noise(key_list[4], (N_SECTION, EXPERTS, D, FF), D ** -0.5, 0.0625, ((0, 8), (1, 8), (3, 4)))
    w_up = noise(key_list[5], (N_SECTION, EXPERTS, D, FF), D ** -0.5, 0.0625, ((0, 8), (1, 8), (3, 4)))
    w_down = noise(key_list[6], (N_SECTION, EXPERTS, FF, D), FF ** -0.5, 0.1875, ((0, 8), (1, 8), (2, 4)))
    return dict(slab=slab, route_ids=route_ids, route_weights=route_weights, norm_gain=norm_gain, w_gate=w_gate, w_up=w_up, w_down=w_down)


def rms_normed(rows, gain):
    values = rows.astype(jnp.float32)
    scale = lax.rsqrt(lax.optimization_barrier(jnp.mean(values * values, axis=-1, keepdims=True)) + 1e-06)
    return (values * scale * gain.astype(jnp.float32)).astype(jnp.bfloat16)

def expert_apply(rows, gate_w, up_w, down_w):
    gate = jnp.dot(rows, gate_w, preferred_element_type=jnp.float32)
    up = jnp.dot(rows, up_w, preferred_element_type=jnp.float32)
    hidden = (jax.nn.silu(gate) * up).astype(jnp.bfloat16)
    count = rows.shape[0]
    slices = hidden.reshape(count, N_TENSOR, FFD).astype(jnp.float32)
    down_parts = down_w.reshape(N_TENSOR, FFD, D).astype(jnp.float32)
    parts = jnp.einsum('mqf,qfd->qmd', slices, down_parts)
    rounded = lax.optimization_barrier(parts.astype(jnp.bfloat16))
    return lax.optimization_barrier(jnp.sum(rounded.astype(jnp.float32), axis=0)).astype(jnp.bfloat16)

def reference(slab, route_ids, route_weights, norm_gain, w_gate, w_up, w_down):
    arriving = jnp.roll(slab, 1, axis=0)
    padded_rows = N_EXPERT * N_TENSOR * CAP
    results = []
    for section in range(N_SECTION):
        rows = arriving[section]
        normed = rms_normed(rows, norm_gain[section])
        ids = route_ids[section].reshape(-1).astype(jnp.int32)
        count = ids.shape[0]
        onehot = (ids[:, None] == jnp.arange(EXPERTS, dtype=jnp.int32)[None, :]).astype(jnp.int32)
        rank = lax.optimization_barrier(jnp.sum((jnp.cumsum(onehot, axis=0) - onehot) * onehot, axis=1)).astype(jnp.int32)
        table = jnp.zeros((EXPERTS, padded_rows), jnp.int32)
        table = table.at[ids, rank].set(jnp.arange(count, dtype=jnp.int32) // TOPK)

        def one_expert(items):
            index_row, gate_w, up_w, down_w = items
            return expert_apply(normed[index_row], gate_w, up_w, down_w)
        outputs = lax.map(one_expert, (table, w_gate[section], w_up[section], w_down[section]))
        picked = outputs[ids, rank].astype(jnp.float32)
        weighted = picked * route_weights[section].reshape(-1)[:, None].astype(jnp.float32)
        mixed = lax.optimization_barrier(jnp.sum(weighted.reshape(TOKENS, TOPK, D), axis=1))
        results.append((rows.astype(jnp.float32) + mixed).astype(jnp.bfloat16))
    return jnp.stack(results, axis=0)
```

```python
import functools
import jax
import jax.numpy as jnp
from jax import lax
from jax.experimental import pallas as pl
from jax.experimental.pallas import tpu as pltpu
from jax.sharding import PartitionSpec as P


def hop(block, axis, distance):
    n = lax.axis_size(axis)
    return lax.ppermute(block, axis, [(i, (i + distance) % n) for i in range(n)])


def across(block):
    return lax.ppermute(block, "tensor", [(0, 2), (1, 3), (2, 0), (3, 1)])


def twin(block):
    return lax.ppermute(block, "tensor", [(0, 1), (1, 0), (2, 3), (3, 2)])


def pick_kernel(count, half, *refs):
    pick_ref, gain_ref = refs[0], refs[1]
    out_ref = refs[-1]
    cap = out_ref.shape[0] // count
    for b in range(count):
        first, second = refs[2 + 2 * b], refs[3 + 2 * b]
        place = pick_ref[b]
        rows = jnp.dot(place[:, :half], first[...], preferred_element_type=jnp.float32)
        rows += jnp.dot(place[:, half:], second[...], preferred_element_type=jnp.float32)
        scale = lax.rsqrt(jnp.mean(rows * rows, axis=-1, keepdims=True) + 1e-06)
        out_ref[b * cap : (b + 1) * cap, :] = (rows * scale * gain_ref[...]).astype(jnp.bfloat16)


def pick_and_norm(place, gain, blocks):
    count, cap, tokens = place.shape
    width = gain.shape[1]
    flat = [piece for block in blocks for piece in block]
    return pl.pallas_call(
        functools.partial(pick_kernel, count, tokens // 2),
        in_specs=[pl.BlockSpec(memory_space=pltpu.VMEM)] * (2 + len(flat)),
        out_specs=pl.BlockSpec(memory_space=pltpu.VMEM),
        out_shape=jax.ShapeDtypeStruct((count * cap, width), jnp.bfloat16),
    )(place, gain, *flat)


def combine_kernel(count, half, *refs):
    share_ref = refs[0]
    first, second = refs[1], refs[2]
    out_ref = refs[-1]
    total = jnp.dot(share_ref[0], refs[3][...], preferred_element_type=jnp.float32)
    for b in range(1, count):
        total += jnp.dot(share_ref[b], refs[3 + b][...], preferred_element_type=jnp.float32)
    total = total[: 2 * half] + total[2 * half :]
    out_ref[:half, :] = (first[...].astype(jnp.float32) + total[:half]).astype(jnp.bfloat16)
    out_ref[half:, :] = (second[...].astype(jnp.float32) + total[half:]).astype(jnp.bfloat16)


def combine(share, rows, blocks):
    count, double, cap = share.shape
    half, width = rows[0].shape
    return pl.pallas_call(
        functools.partial(combine_kernel, count, half),
        in_specs=[pl.BlockSpec(memory_space=pltpu.VMEM)] * (3 + count),
        out_specs=pl.BlockSpec(memory_space=pltpu.VMEM),
        out_shape=jax.ShapeDtypeStruct((2 * half, width), jnp.bfloat16),
    )(share, *rows, *blocks)


def slots_of(named, cap):
    tokens = named.shape[1]
    before = (jnp.arange(tokens)[:, None] < jnp.arange(tokens)[None, :]).astype(jnp.float32)
    rank = jnp.dot(named, before, preferred_element_type=jnp.float32)
    slot = jnp.arange(cap, dtype=jnp.float32)[None, :, None]
    return jnp.where(slot == rank[:, None, :], named[:, None, :], 0.0)


OFFSETS = (0, -1, 1, -2, 2, -3, 3, 4)


def local(slab, route_ids, route_weights, norm_gain, w_gate, w_up, w_down):
    tokens = slab.shape[1]
    width = slab.shape[2]
    half = tokens // 2
    owners = lax.axis_size("expert")
    cap = 2 * tokens * route_ids.shape[2] // owners
    me = lax.axis_index("expert")
    x = slab[0]
    held = {0: (hop(x[:half], "section", 1), hop(x[half:], "section", 1))}
    gates = (w_gate[0, 0], twin(w_gate[0, 0]))
    ups = (w_up[0, 0], twin(w_up[0, 0]))
    downs = (w_down[0, 0], twin(w_down[0, 0]))
    ids = route_ids[0]
    everyone = lax.all_to_all(
        jnp.broadcast_to(ids.reshape(1, -1), (owners, ids.size)), "expert", 0, 0, tiled=True
    ).reshape(owners, tokens, -1)
    order = jnp.asarray(OFFSETS, jnp.int32)
    near = everyone[(me + order) % owners]
    mine = jnp.any(near == me, axis=2).astype(jnp.float32)
    place = slots_of(mine, cap).astype(jnp.bfloat16)
    senders = ((me - order) % owners)[:, None, None]
    hits = (ids[None] == senders).astype(jnp.float32)
    share = slots_of(jnp.sum(hits, axis=2), cap) * jnp.sum(hits * route_weights[0][None], axis=2)[:, None, :]
    share = jnp.transpose(share, (0, 2, 1))
    high = share.astype(jnp.bfloat16)
    low = (share - high.astype(jnp.float32)).astype(jnp.bfloat16)
    share = jnp.concatenate([high, low], axis=1)

    for j in (1, 2, 3):
        held[-j] = tuple(hop(piece, "expert", 1) for piece in held[1 - j])
        held[j] = tuple(hop(piece, "expert", -1) for piece in held[j - 1])
    held[4] = (hop(held[-3][0], "expert", 1), hop(held[3][1], "expert", -1))

    groups = ((0,), (-1, 1), (-2, 2), (-3, 3), (4,))
    gain = norm_gain
    own, other = [], []
    for g in groups:
        at = [OFFSETS.index(o) for o in g]
        picked = pick_and_norm(place[at[0] : at[-1] + 1], gain, [held[o] for o in g])
        own.append(picked)
        other.append(across(picked))

    def hidden_of(rows):
        result = []
        for gate_w, up_w in zip(gates, ups):
            gate = jnp.dot(rows, gate_w, preferred_element_type=jnp.float32)
            up = jnp.dot(rows, up_w, preferred_element_type=jnp.float32)
            result.append((jax.nn.silu(gate) * up).astype(jnp.bfloat16))
        return result

    parts = {}
    for batch in ((0, 1, 2), (3, 4)):
        rows = jnp.concatenate([piece for k in batch for piece in (own[k], other[k])], axis=0)
        hidden = hidden_of(rows)
        start = 0
        for k in batch:
            n = own[k].shape[0]
            parts[k] = [h[start : start + 2 * n] for h in hidden]
            start += 2 * n

    arrived = {}
    for k in (4, 3, 2, 1, 0):
        n = own[k].shape[0]

        def down(lo, hi):
            total = jnp.dot(parts[k][0][lo:hi], downs[0], preferred_element_type=jnp.float32)
            return total + jnp.dot(parts[k][1][lo:hi], downs[1], preferred_element_type=jnp.float32)

        sent = across(down(n, 2 * n).astype(jnp.bfloat16))
        outs = (down(0, n) + sent.astype(jnp.float32)).astype(jnp.bfloat16)
        for i, o in enumerate(groups[k]):
            piece = outs[i * cap : (i + 1) * cap]
            arrived[o] = piece if o == 0 else hop(piece, "expert", o)
    return combine(share, held[0], [arrived[o] for o in OFFSETS])[None]


def solution(mesh):
    return jax.shard_map(
        local,
        mesh=mesh,
        in_specs=(
            P("section", ("expert", "tensor"), None),
            P("section", ("expert", "tensor"), None),
            P("section", ("expert", "tensor"), None),
            P("section", None),
            P("section", "expert", None, "tensor"),
            P("section", "expert", None, "tensor"),
            P("section", "expert", "tensor", None),
        ),
        out_specs=P("section", ("expert", "tensor"), None),
        check_vma=False,
    )
```
